32 devices in a mesh: island: 2 (over x), row: 4 (over y, core), col: 4 (over z).
Axes of the slice: x: 2, y: 2, z: 4, core: 2. Of those that a mesh axis runs over, the one named last changes fastest.
Arguments:
- deltas: float32 [2, 4096, 8192], P('island', 'row', 'col'), may hold values from -0.13258252 to 0.13258252
- left_stat: float32 [4096, 4096], P(('island', 'col'), 'row'), may hold values from -1.5 to 1.5
- right_stat: float32 [8192, 8192], P(('island', 'row'), 'col'), may hold values from -1.5 to 1.5
Outputs:
- left_new: float32 [4096, 4096], P(('island', 'col'), 'row')
- right_new: float32 [8192, 8192], P(('island', 'row'), 'col')
The draws below stay inside these ranges and needn't reach their ends.
All inputs are finite; a program needn't handle non-finite values.
Results may differ from the reference program's by a relative error of at most 0.00037.
Values may be sent and summed in bfloat16 or wider, within the bound.
A program may use at most 128 MiB of HBM per device.

```python
import jax
import jax.numpy as jnp
from jax import lax

M = 4096
N = 8192
ISLANDS = 2


def steps_of(own_key, dims, split, smallest, high):
    loudness = 1.0
    for position, shards_of in split:
        draws = jax.random.uniform(jax.random.fold_in(jax.random.fold_in(own_key, 6), position), (shards_of,), jnp.float32, smallest / len(split), high / len(split))
        loudness = loudness * jnp.repeat(jnp.exp(draws), dims[position] // shards_of).reshape((-1,) + (1,) * (len(dims) - 1 - position))
    return loudness


def noise(key, extent, deviation, limit, shards=(), dtype=jnp.bfloat16):
    drawn = jax.random.normal(key, extent, jnp.float32) * deviation
    if len(shards) > 0:
        drawn = steps_of(key, extent, shards, -0.22, 0.18) * drawn
    return jnp.clip(drawn, min=-limit, max=limit).astype(dtype)


def setup_inputs(seed: int = 0) -> dict:
    seeds = jax.random.split(jax.random.key(seed), 4)
    deltas = noise(seeds[0], (ISLANDS, M, N), ((ISLANDS / M) ** 0.5), 0.13258252, ((0, 2), (1, 4), (2, 4)), jnp.float32)
    left_stat = noise(seeds[1], (M, M), 0.25, 1.5, ((0, 8), (1, 4)), jnp.float32)
    right_stat = noise(seeds[2], (N, N), 0.25, 1.5, ((0, 8), (1, 4)), jnp.float32)
    return dict(deltas=deltas, left_stat=left_stat, right_stat=right_stat)


def reference(deltas, left_stat, right_stat):
    outer_grad = jnp.sum(deltas, axis=0) / deltas.shape[0]
    rounded = lax.optimization_barrier(outer_grad.astype(jnp.bfloat16)).astype(jnp.float32)
    left_gram = jnp.dot(rounded, rounded.T, precision=lax.Precision.HIGHEST, preferred_element_type=jnp.float32)
    right_gram = jnp.dot(rounded.T, rounded, precision=lax.Precision.HIGHEST, preferred_element_type=jnp.float32)
    return left_stat + left_gram, right_stat + right_gram
```

```python
import functools

import jax
import jax.numpy as jnp
from jax import lax
from jax.experimental import pallas as pl
from jax.experimental.pallas import tpu as pltpu
from jax.sharding import PartitionSpec as P

CHUNKS = 8
AHEAD = 2
MESH = pl.DeviceIdType.MESH


def gather_kernel(
    islands, rows, cols, chunks,
    delta_ref, strip_ref, block_ref,
    own_v, got_v, out_v, load_sem, store_sem, send_sem, recv_sem,
):
    i, r, c = lax.axis_index("island"), lax.axis_index("row"), lax.axis_index("col")
    step_rows = delta_ref.shape[1] // chunks
    width = block_ref.shape[2]
    per_strip = islands * rows // cols
    number = i * rows + r
    home, part = number // per_strip, number % per_strip
    x_peer = {"island": 1 - i}
    far_row = (r + 2) % 4
    core_row = r + 1 - 2 * (r % 2)
    y_peer, core_peer = {"row": far_row}, {"row": core_row}
    up, down = {"col": c + 1}, {"col": c - 1}
    has_up, has_down = c < cols - 1, c > 0
    hops = jnp.abs(c - home)
    lag = jnp.maximum(hops, 1)

    def at(j):
        return pl.ds(pl.multiple_of(j * step_rows, step_rows), step_rows)

    def remote(src, dst, flow, j, peer, arrival=None):
        return pltpu.make_async_remote_copy(
            src_ref=src, dst_ref=dst,
            send_sem=send_sem.at[flow, j],
            recv_sem=recv_sem.at[flow if arrival is None else arrival, j],
            device_id=peer, device_id_type=MESH,
        )

    def x_wide(j):
        return remote(delta_ref.at[1 - i, at(j)], got_v.at[j], 0, j, x_peer)

    def x_round(j, half):
        piece = strip_ref.at[2 * r + half, at(j)]
        return remote(piece, piece, 1, j, x_peer)

    def slabs(row, flow, j, peer):
        piece = strip_ref.at[pl.ds(2 * row, 2), at(j)]
        return remote(piece, piece, flow, j, peer)

    def columns(which):
        return pl.ds(pl.multiple_of(which * width, width), width)

    def z_core(j):
        other = per_strip - 1 - part
        return remote(strip_ref.at[:, at(j), columns(other)], block_ref.at[:, at(j)], 5, j, core_peer)

    def z_first(j, flow, peer):
        return remote(strip_ref.at[:, at(j), columns(part)], block_ref.at[:, at(j)], flow, j, peer, 5)

    def z_next(j, flow, peer):
        return remote(block_ref.at[:, at(j)], block_ref.at[:, at(j)], flow, j, peer, 5)

    barrier = pltpu.get_barrier_semaphore()
    for peer in (x_peer, y_peer, core_peer):
        pl.semaphore_signal(barrier, inc=1, device_id=peer, device_id_type=MESH)

    @pl.when(has_up)
    def _():
        pl.semaphore_signal(barrier, inc=1, device_id=up, device_id_type=MESH)

    @pl.when(has_down)
    def _():
        pl.semaphore_signal(barrier, inc=1, device_id=down, device_id_type=MESH)

    load = pltpu.make_async_copy(delta_ref.at[i], own_v, load_sem)
    load.start()
    pl.semaphore_wait(barrier, 3 + has_up.astype(jnp.int32) + has_down.astype(jnp.int32))
    for j in range(min(AHEAD, chunks)):
        x_wide(j).start()
    load.wait()

    def inside(j):
        return jnp.logical_and(j >= 0, j < chunks)

    def step(t, _):
        @pl.when(t < chunks)
        def _():
            x_wide(t).wait_recv()
            out_v[t] = ((own_v[at(t)] + got_v[t]) / islands).astype(jnp.bfloat16)
            store = pltpu.make_async_copy(out_v.at[t], strip_ref.at[2 * r + i, at(t)], store_sem)
            store.start()
            store.wait()
            x_round(t, i).start()

        @pl.when(t + AHEAD < chunks)
        def _():
            x_wide(t + AHEAD).start()

        @pl.when(inside(t - 1))
        def _():
            x_round(t - 1, 1 - i).wait_recv()
            slabs(r, 2, t - 1, y_peer).start()
            slabs(r, 3, t - 1, core_peer).start()

        @pl.when(inside(t - 2))
        def _():
            slabs(far_row, 2, t - 2, y_peer).wait_recv()
            slabs(far_row, 4, t - 2, core_peer).start()

        @pl.when(inside(t - 3))
        def _():
            slabs(core_row, 3, t - 3, core_peer).wait_recv()
            slabs((core_row + 2) % 4, 4, t - 3, core_peer).wait_recv()

            @pl.when(hops == 0)
            def _():
                z_core(t - 3).start()

                @pl.when(has_up)
                def _():
                    z_first(t - 3, 6, up).start()

                @pl.when(has_down)
                def _():
                    z_first(t - 3, 7, down).start()

        late = t - 3 - lag

        @pl.when(inside(late))
        def _():
            z_core(late).wait_recv()

            @pl.when(jnp.logical_and(c > home, has_up))
            def _():
                z_next(late, 6, up).start()

            @pl.when(jnp.logical_and(c < home, has_down))
            def _():
                z_next(late, 7, down).start()

        return 0

    lax.fori_loop(0, chunks + 2 + cols, step, 0)

    def finish(j, _):
        x_wide(j).wait_send()
        x_round(j, i).wait_send()
        slabs(r, 2, j, y_peer).wait_send()
        slabs(r, 3, j, core_peer).wait_send()
        slabs(far_row, 4, j, core_peer).wait_send()

        @pl.when(hops == 0)
        def _():
            z_core(j).wait_send()

        @pl.when(jnp.logical_and(c >= home, has_up))
        def _():
            z_next(j, 6, up).wait_send()

        @pl.when(jnp.logical_and(c <= home, has_down))
        def _():
            z_next(j, 7, down).wait_send()

        return 0

    lax.fori_loop(0, chunks, finish, 0)


def gather(delta, islands, rows, cols):
    share, wide = delta.shape[0] // islands, delta.shape[1]
    width = wide * cols // (islands * rows)
    step_rows = share // CHUNKS
    strip, block = pl.pallas_call(
        functools.partial(gather_kernel, islands, rows, cols, CHUNKS),
        out_shape=(
            jax.ShapeDtypeStruct((rows * islands, share, wide), jnp.bfloat16),
            jax.ShapeDtypeStruct((rows * islands, share, width), jnp.bfloat16),
        ),
        in_specs=[pl.BlockSpec(memory_space=pl.ANY)],
        out_specs=(pl.BlockSpec(memory_space=pl.ANY), pl.BlockSpec(memory_space=pl.ANY)),
        scratch_shapes=[
            pltpu.VMEM((share, wide), jnp.float32),
            pltpu.VMEM((CHUNKS, step_rows, wide), jnp.float32),
            pltpu.VMEM((CHUNKS, step_rows, wide), jnp.bfloat16),
            pltpu.SemaphoreType.DMA,
            pltpu.SemaphoreType.DMA,
            pltpu.SemaphoreType.DMA((8, CHUNKS)),
            pltpu.SemaphoreType.DMA((8, CHUNKS)),
        ],
        compiler_params=pltpu.CompilerParams(collective_id=0, has_side_effects=True),
    )(delta.reshape(islands, share, wide))
    return strip.reshape(-1, wide), block.reshape(-1, width)


def paired(deltas, left_stat, right_stat):
    islands, rows, cols = (lax.axis_size(name) for name in ("island", "row", "col"))
    c = lax.axis_index("col")
    strip, block = gather(deltas[0], islands, rows, cols)
    features = strip.shape[0]
    extent = left_stat.shape[0]
    plane = jnp.concatenate(
        [
            lax.dynamic_slice_in_dim(block, n * (features // islands) + c * extent, extent, 0)
            for n in range(islands)
        ],
        axis=0,
    )
    tall = features // rows
    tiles = [
        lax.dot_general(
            plane, block[n * tall:(n + 1) * tall], (((1,), (1,)), ((), ())),
            preferred_element_type=jnp.float32,
        )
        for n in range(rows)
    ]
    by_row = lax.psum_scatter(jnp.concatenate(tiles, axis=0), "row", scatter_dimension=0, tiled=True)
    left_new = left_stat + lax.psum_scatter(by_row, "island", scatter_dimension=0, tiled=True)
    right_new = right_stat + lax.dot_general(
        block, strip, (((0,), (0,)), ((), ())), preferred_element_type=jnp.float32
    )
    return left_new, right_new


def broadcast(value, axis, source):
    kept = jnp.where(lax.axis_index(axis) == source, value, 0).astype(value.dtype)
    return lax.psum(kept, axis)


def general(deltas, left_stat, right_stat):
    islands = lax.axis_size("island")
    row_count = lax.axis_size("row")
    island = lax.axis_index("island")
    local_delta = deltas[0]
    shares = lax.psum_scatter(local_delta, "island", scatter_dimension=0, tiled=True)
    rounded = (shares / islands).astype(jnp.bfloat16)
    panel = lax.all_gather(rounded, "island", axis=0, tiled=True)
    rows_local = panel.shape[0]
    rows_island = rows_local * row_count // islands
    row_pieces = max(1, row_count // islands)
    row_extent = min(rows_island, rows_local)
    blocks = []
    for number in range(row_pieces):
        start_row = island * rows_island + number * row_extent
        blocks.append(broadcast(panel, "row", start_row // rows_local))
    left_block = jnp.concatenate(blocks, axis=0)
    left_tile = lax.dot_general(
        left_block, panel, (((1,), (1,)), ((), ())), preferred_element_type=jnp.float32
    )
    left_shares = lax.psum_scatter(left_tile, "col", scatter_dimension=0, tiled=True)
    left_new = left_stat + left_shares
    cols_island = panel.shape[1] * lax.axis_size("col") // islands
    whole_rows = lax.all_gather(panel, "col", axis=1, tiled=True)
    right_block = lax.dynamic_slice_in_dim(whole_rows, island * cols_island, cols_island, 1)
    right_tile = lax.dot_general(
        right_block, panel, (((0,), (0,)), ((), ())), preferred_element_type=jnp.float32
    )
    right_shares = lax.psum_scatter(right_tile, "row", scatter_dimension=0, tiled=True)
    right_new = right_stat + right_shares
    return (left_new, right_new)


def solution(mesh):
    in_specs = (P("island", "row", "col"), P(("island", "col"), "row"), P(("island", "row"), "col"))
    out_specs = (P(("island", "col"), "row"), P(("island", "row"), "col"))
    sizes = mesh.shape
    fits = sizes["island"] == 2 and sizes["row"] == 4 and sizes["island"] * sizes["row"] == 2 * sizes["col"]
    local = paired if fits else general
    return jax.shard_map(local, mesh=mesh, in_specs=in_specs, out_specs=out_specs, check_vma=False)
```
